32 devices in a mesh: dp: 4 (over y, core), attn: 8 (over z, x).
Axes of the slice: x: 2, y: 2, z: 4, core: 2. Of those that a mesh axis runs over, the one named last changes fastest.
Arguments:
- query_states: bfloat16 [4096, 4096], P(('dp', 'attn')), may hold values from -96 to 96
- key_states: bfloat16 [4096, 512], P(('dp', 'attn')), may hold values from -4.5 to 4.5
- value_states: bfloat16 [4096, 512], P(('dp', 'attn')), may hold values from -6 to 6
- out_grad: bfloat16 [4096, 4096], P(('dp', 'attn')), may hold values from -24 to 24
- doc_lengths: int32 [4, 12], P('dp'), may hold values from 1 to 384, 1024 in all within a row
- layer_inputs: bfloat16 [4096, 4096], P(None, ('dp', 'attn')), may hold values from -8 to 8
Outputs:
- query_grad: bfloat16 [4096, 4096], P(('dp', 'attn'))
- weight_grad: float32 [4096, 1024], P(('dp', 'attn'))
The draws below stay inside these ranges and needn't reach their ends.
Inputs may be any that keep to these rules, and one draw needn't show every extreme that they name: `doc_lengths`: row g lists the lengths of the documents of data group g in the order in which they lie in its pack; they sum to 1024, and the longest is exactly 384.
All inputs are finite; a program needn't handle non-finite values.
Results may differ from the reference program's by a relative error of at most 0.0051.
Values may be sent and summed in bfloat16 or wider, within the bound.
No kernel may reach another device: no remote copies, remote signals or barrier semaphores. Data moves between devices by JAX's collectives and lax.ppermute only.
A program may use at most 64 MiB of HBM per device.

```python
import math
import jax
import jax.numpy as jnp
import numpy as np
from jax import lax

D = 4096
HQ = 32
KVH = 4
DH = 128
GROUP = 8
TOK_DEV = 128
NDOC = 12
MOST = 384
GROUP_TOK = 1024
TOKENS = 4096
N_DP = 4


def paired_draw(key):
    key_base = jax.random.fold_in(key, 11)
    query_base = jax.random.fold_in(key, 12)
    base_keys = jnp.clip(jax.random.normal(key_base, (TOKENS, KVH * DH), jnp.float32), -4.0, 4.0)
    base_queries = jnp.clip(jax.random.normal(query_base, (TOKENS, HQ * DH), jnp.float32), -4.0, 4.0)
    keys_out = base_keys
    queries_out = base_queries
    return (queries_out, keys_out)


def draw_query_states(key, part):
    queries_out, keys_out = paired_draw(key)
    return queries_out.astype(jnp.bfloat16)


def draw_key_states(key, part):
    queries_out, keys_out = paired_draw(key)
    return keys_out.astype(jnp.bfloat16)


def with_spikes(result, own_key, source, target, blocks, factor):
    owner, partner = [(jnp.arange(result.shape[dim]) // (result.shape[dim] // blocks)).reshape([-1 if axis == dim else 1 for axis in range(result.ndim)]) for dim in (source, target)]
    chosen = jax.random.permutation(own_key, blocks)[partner]
    strong = (owner == chosen) | (owner == (partner + blocks // 2) % blocks)
    return jnp.where(strong, factor * result, result)


def shard_levels(rng, dims, pieces, least, high):
    gain = 1.0
    for axis_at, blocks in pieces:
        draws = jax.random.uniform(jax.random.fold_in(jax.random.fold_in(rng, 6), axis_at), (blocks,), jnp.float32, least / len(pieces), high / len(pieces))
        gain = gain * jnp.repeat(jnp.exp(draws), dims[axis_at] // blocks).reshape((-1,) + (1,) * (len(dims) - 1 - axis_at))
    return gain


def length_profile(number_of, total, reach, lean):
    portions = [(1 << 20) // math.isqrt(rank ** lean) + 1 for rank in range(2, number_of + 1)]
    spare, holding = total - reach - (number_of - 1), [1] * (number_of - 1)
    while spare > 0:
        candidates = [i for i in range(number_of - 1) if holding[i] < reach]
        mass, remaining = sum([portions[i] for i in candidates]), spare
        for i in candidates:
            more = min(reach - holding[i], max(1, remaining * portions[i] // mass), spare)
            holding[i] = holding[i] + more
            spare = spare - more
    return np.array([reach] + holding)


def uneven_parts(key, number_of, total, limit, skew):
    if number_of == 2:
        one = jax.random.randint(key, (), max(1, total - limit), min(limit, total - 1) + 1)
        return jnp.stack([one, total - one])
    tallies = jnp.asarray(length_profile(number_of, total, limit, skew), jnp.int32)
    pairs = (number_of - 1) // 2
    donor, receiver = tallies[1:1 + 2 * pairs:2], tallies[2:2 + 2 * pairs:2]
    room = jnp.minimum(donor - 1, limit - receiver)
    shifted = jax.random.randint(jax.random.fold_in(key, 1), (pairs,), 0, 1 << 20) % (room + 1)
    tallies = tallies.at[1:1 + 2 * pairs:2].set(donor - shifted).at[2:2 + 2 * pairs:2].set(receiver + shifted)
    return tallies[jax.random.permutation(jax.random.fold_in(key, 2), number_of)]


def gaussian(key, dims, width, limit, pieces=(), kind=jnp.bfloat16):
    array = jax.random.normal(key, dims, jnp.float32) * width
    if len(pieces) > 0:
        array = shard_levels(key, dims, pieces, -0.22, 0.18) * array
    return jnp.clip(array, min=-limit, max=limit).astype(kind)


def bell_draw_with(stream_key, extent, deviation, reach, shards, heavy, kind=jnp.bfloat16):
    result = deviation * jax.random.normal(stream_key, extent, jnp.float32)
    if shards:
        result = result * shard_levels(stream_key, extent, shards, -0.22, 0.18)
    return jnp.clip(with_spikes(result, jax.random.fold_in(stream_key, 3), *heavy), -reach, reach).astype(kind)


def setup_inputs(seed: int = 0) -> dict:
    arg_keys = jax.random.split(jax.random.key(seed), 7)
    query_states = draw_query_states(jax.random.fold_in(arg_keys[6], 71), 0)
    key_states = draw_key_states(jax.random.fold_in(arg_keys[6], 71), 0)
    value_states = gaussian(arg_keys[2], (TOKENS, KVH * DH), 1.0, 6.0, ((0, 32),))
    out_grad = gaussian(arg_keys[3], (TOKENS, HQ * DH), 4.0, 24.0, ((0, 32),))
    doc_lengths = jax.vmap(lambda own: uneven_parts(own, NDOC, GROUP_TOK, MOST, 2))(jax.random.split(arg_keys[4], N_DP)).reshape((N_DP, NDOC)).astype(jnp.int32)
    layer_inputs = bell_draw_with(arg_keys[5], (D, TOKENS), 1.0, 8.0, ((1, 32),), (1, 0, 32, 2.75))
    return dict(query_states=query_states, key_states=key_states, value_states=value_states, out_grad=out_grad, doc_lengths=doc_lengths, layer_inputs=layer_inputs)


masked_score = -1e30


def doc_index(position, bounds):
    return jnp.sum((position[:, None] >= bounds[None, :]).astype(jnp.int32), axis=1).astype(jnp.int32)


def group_grads(group_queries, group_keys, group_values, group_out, lengths):
    bounds = jnp.cumsum(lengths).astype(jnp.int32)
    padding = jnp.zeros((MOST, KVH * DH), group_keys.dtype)
    key_padded = jnp.concatenate([padding, group_keys], axis=0)
    value_padded = jnp.concatenate([padding, group_values], axis=0)
    score_scale = DH ** -0.5
    window = TOK_DEV + MOST

    def one_block(running, block_index):
        first_row = (block_index * TOK_DEV).astype(jnp.int32)
        query_block = lax.dynamic_slice_in_dim(group_queries, first_row, TOK_DEV, 0).astype(jnp.float32).reshape(TOK_DEV, KVH, GROUP, DH)
        grad_block = lax.dynamic_slice_in_dim(group_out, first_row, TOK_DEV, 0).astype(jnp.float32).reshape(TOK_DEV, KVH, GROUP, DH)
        key_window = lax.dynamic_slice_in_dim(key_padded, first_row, window, 0).astype(jnp.float32).reshape(window, KVH, DH)
        value_window = lax.dynamic_slice_in_dim(value_padded, first_row, window, 0).astype(jnp.float32).reshape(window, KVH, DH)
        query_pos = first_row + jnp.arange(TOK_DEV, dtype=jnp.int32)
        key_pos = first_row - MOST + jnp.arange(window, dtype=jnp.int32)
        allowed = (key_pos[None, :] >= 0) & (key_pos[None, :] <= query_pos[:, None])
        allowed = allowed & (doc_index(query_pos, bounds)[:, None] == doc_index(key_pos, bounds)[None, :])
        scores = score_scale * jnp.einsum("tgjd,ugd->gjtu", query_block, key_window)
        scores = jnp.where(allowed, scores, masked_score)
        row_max = jnp.max(scores, axis=-1, keepdims=True)
        weights = jnp.exp(scores - row_max)
        probs = weights / jnp.sum(weights, axis=-1, keepdims=True)
        dprobs = jnp.einsum("tgjd,ugd->gjtu", grad_block, value_window)
        row_delta = jnp.sum(probs * dprobs, axis=-1, keepdims=True)
        dscores = lax.optimization_barrier((probs * (dprobs - row_delta)).astype(jnp.bfloat16)).astype(jnp.float32)
        probs_low = lax.optimization_barrier(probs.astype(jnp.bfloat16)).astype(jnp.float32)
        query_grad = (score_scale * jnp.einsum("gjtu,ugd->tgjd", dscores, key_window)).astype(jnp.bfloat16)
        key_grad = score_scale * jnp.einsum("gjtu,tgjd->ugd", dscores, query_block)
        value_grad = jnp.einsum("gjtu,tgjd->ugd", probs_low, grad_block)
        both = jnp.stack([key_grad, value_grad]).reshape(2, window, KVH * DH)
        current = lax.dynamic_slice_in_dim(running, first_row, window, 1)
        running = lax.dynamic_update_slice_in_dim(running, current + both, first_row, 1)
        return running, query_grad.reshape(TOK_DEV, HQ * DH)

    initial = jnp.zeros((2, GROUP_TOK + MOST, KVH * DH), jnp.float32)
    totals, query_grads = lax.scan(one_block, initial, jnp.arange(GROUP_TOK // TOK_DEV, dtype=jnp.int32))
    kv_rows = jnp.concatenate([totals[0, MOST:], totals[1, MOST:]], axis=1).astype(jnp.bfloat16)
    return query_grads.reshape(GROUP_TOK, HQ * DH), kv_rows


def reference(query_states, key_states, value_states, out_grad, doc_lengths, layer_inputs):
    def per_group(running, group_index):
        first_row = (group_index * GROUP_TOK).astype(jnp.int32)
        group_queries = lax.dynamic_slice_in_dim(query_states, first_row, GROUP_TOK, 0)
        group_keys = lax.dynamic_slice_in_dim(key_states, first_row, GROUP_TOK, 0)
        group_values = lax.dynamic_slice_in_dim(value_states, first_row, GROUP_TOK, 0)
        group_out = lax.dynamic_slice_in_dim(out_grad, first_row, GROUP_TOK, 0)
        lengths = lax.dynamic_index_in_dim(doc_lengths, group_index, 0, keepdims=False)
        query_grad, kv_rows = group_grads(group_queries, group_keys, group_values, group_out, lengths)
        group_inputs = lax.dynamic_slice_in_dim(layer_inputs, first_row, GROUP_TOK, 1)
        running = running + jnp.dot(group_inputs, kv_rows, preferred_element_type=jnp.float32)
        return running, query_grad

    initial = jnp.zeros((D, 2 * KVH * DH), jnp.float32)
    weight_total, query_grads = lax.scan(per_group, initial, jnp.arange(N_DP, dtype=jnp.int32))
    return query_grads.reshape(TOKENS, HQ * DH), weight_total * (float(TOKENS) ** -0.5)
```

```python
from functools import partial

import jax
import jax.numpy as jnp
from jax import lax
from jax.experimental import pallas as pl
from jax.experimental.pallas import tpu as pltpu
from jax.sharding import PartitionSpec as P

DH = 128
SPAN = 3
CHUNKS = 1
LOG2E = 1.4426950408889634

masked_score = -1e30


def passed_along(shard, axis, by):
    size = lax.axis_size(axis)
    pairs = [(i, i + by) for i in range(size) if 0 <= i + by < size]
    return lax.ppermute(shard, axis, pairs)


class Grid:
    def __init__(self, attn_size, data_size):
        self.attn = attn_size
        self.data = data_size
        self.lo = 2 if attn_size % 2 == 0 else 1
        self.hi = attn_size // self.lo
        self.inner = 2 if data_size % 2 == 0 else 1
        self.outer = data_size // self.inner

    def index(self, outer, inner, hi, lo):
        return (outer * self.inner + inner) * self.attn + hi * self.lo + lo

    def rotated(self, value, outer=0, inner=0, hi=0, lo=0):
        pairs = []
        for o in range(self.outer):
            for i in range(self.inner):
                for h in range(self.hi):
                    for l in range(self.lo):
                        target = self.index(
                            (o + outer) % self.outer,
                            (i + inner) % self.inner,
                            (h + hi) % self.hi,
                            (l + lo) % self.lo,
                        )
                        pairs.append((self.index(o, i, h, l), target))
        return lax.ppermute(value, ("dp", "attn"), pairs)


def attention_kernel(
    lengths, q_ref, g_ref, *refs, chunk_heads, rows_dev, members, score_scale
):
    kv_refs = refs[: SPAN + 1]
    dq_ref, own_ref = refs[-(SPAN + 5) : -(SPAN + 3)]
    part_refs = refs[-(SPAN + 3) : -3]
    bias_ref, ds_ref, p_ref = refs[-3:]
    head_size = DH
    wide = 2 * rows_dev
    key_at = lax.broadcasted_iota(jnp.int32, (rows_dev, wide), 0)
    query_at = lax.broadcasted_iota(jnp.int32, (rows_dev, wide), 1) % rows_dev
    causal = key_at <= query_at

    @pl.when(pl.program_id(0) == 0)
    def _():
        base = lax.axis_index("attn") * rows_dev
        start = jnp.zeros((rows_dev, wide), jnp.int32)
        bound = jnp.int32(0)
        for doc in range(lengths.shape[1]):
            bound = bound + lengths[0, doc]
            start = jnp.where(query_at + base >= bound, bound, start)
        start = start - base
        merged_at = jnp.where(causal, key_at, key_at - SPAN * rows_dev)
        bias_ref[0:rows_dev, :] = jnp.where(merged_at >= start, 0.0, masked_score)
        for offset in range(1, SPAN):
            visible = key_at - offset * rows_dev >= start
            bias_ref[offset * rows_dev : (offset + 1) * rows_dev, :] = jnp.where(
                visible, 0.0, masked_score
            )

    keys = jnp.concatenate([ref[:, :head_size] for ref in kv_refs], axis=0)
    values = jnp.concatenate([ref[:, head_size:] for ref in kv_refs], axis=0)
    keys_turned = keys.T
    last_dims = (((1,), (1,)), ((), ()))

    def head(ref, j):
        return ref[:, j * head_size : (j + 1) * head_size]

    def block(array, offset):
        return array[offset * rows_dev : (offset + 1) * rows_dev, :]

    for pair in range(members // 2):
        q_two = jnp.concatenate([head(q_ref, 2 * pair), head(q_ref, 2 * pair + 1)], axis=0)
        g_two = jnp.concatenate([head(g_ref, 2 * pair), head(g_ref, 2 * pair + 1)], axis=0)
        scores = lax.dot_general(keys, q_two, last_dims, preferred_element_type=jnp.float32)
        dprobs = lax.dot_general(values, g_two, last_dims, preferred_element_type=jnp.float32)
        s = [jnp.where(causal, block(scores, 0), block(scores, SPAN))]
        d = [jnp.where(causal, block(dprobs, 0), block(dprobs, SPAN))]
        for offset in range(1, SPAN):
            s.append(block(scores, offset))
            d.append(block(dprobs, offset))
        s = jnp.concatenate(s, axis=0) + bias_ref[...]
        d = jnp.concatenate(d, axis=0)
        top = jnp.max(s, axis=0, keepdims=True)
        e = jnp.exp2((s - top) * (score_scale * LOG2E))
        inverse = 1.0 / jnp.sum(e, axis=0, keepdims=True)
        probs = e * inverse
        delta = jnp.sum(probs * d, axis=0, keepdims=True)
        ds = probs * (d - delta)
        columns = slice(pair * wide, (pair + 1) * wide)
        for target, full in ((ds_ref, ds), (p_ref, probs)):
            merged = block(full, 0)
            target[0:rows_dev, columns] = jnp.where(causal, merged, 0.0).astype(jnp.bfloat16)
            target[SPAN * rows_dev :, columns] = jnp.where(causal, 0.0, merged).astype(
                jnp.bfloat16
            )
            target[rows_dev : SPAN * rows_dev, columns] = full[rows_dev:, :].astype(jnp.bfloat16)
        dq_turned = score_scale * jnp.dot(
            keys_turned, ds_ref[:, columns], preferred_element_type=jnp.float32
        )
        for k in range(2):
            j = 2 * pair + k
            dq_ref[:, j * head_size : (j + 1) * head_size] = dq_turned[
                :, k * rows_dev : (k + 1) * rows_dev
            ].T.astype(jnp.bfloat16)

    q_all = jnp.concatenate([head(q_ref, j) for j in range(members)], axis=0)
    g_all = jnp.concatenate([head(g_ref, j) for j in range(members)], axis=0)
    dk = score_scale * jnp.dot(ds_ref[...], q_all, preferred_element_type=jnp.float32)
    dv = jnp.dot(p_ref[...], g_all, preferred_element_type=jnp.float32)
    own_ref[:, :head_size] = block(dk, 0)
    own_ref[:, head_size:] = block(dv, 0)
    for offset in range(1, SPAN + 1):
        part = part_refs[offset - 1]
        part[:, :head_size] = block(dk, offset).astype(jnp.bfloat16)
        part[:, head_size:] = block(dv, offset).astype(jnp.bfloat16)


def attention(chunk, lengths, queries, out_grads, kv_blocks, previous):
    rows_dev, width = queries.shape
    chunk_heads = kv_blocks[0].shape[1] // (2 * DH)
    members = width // (chunk_heads * CHUNKS * DH)
    first = chunk * chunk_heads
    wide_spec = pl.BlockSpec((rows_dev, members * DH), lambda h: (0, first + h))
    kv_spec = pl.BlockSpec((rows_dev, 2 * DH), lambda h: (0, h))
    in_specs = [pl.BlockSpec(memory_space=pltpu.SMEM), wide_spec, wide_spec]
    in_specs += [kv_spec] * (SPAN + 1)
    operands = [lengths, queries, out_grads, *kv_blocks]
    aliases = {}
    if previous is not None:
        aliases = {len(operands): 0}
        in_specs.append(pl.BlockSpec(memory_space=pl.ANY))
        operands.append(previous)
    pair = (rows_dev, chunk_heads * 2 * DH)
    window = (SPAN + 1) * rows_dev
    elements = chunk_heads * members * rows_dev * window
    return pl.pallas_call(
        partial(
            attention_kernel,
            chunk_heads=chunk_heads,
            rows_dev=rows_dev,
            members=members,
            score_scale=DH ** (-0.5),
        ),
        grid=(chunk_heads,),
        in_specs=in_specs,
        out_specs=[wide_spec] + [kv_spec] * (SPAN + 1),
        out_shape=[jax.ShapeDtypeStruct((rows_dev, width), jnp.bfloat16)]
        + [jax.ShapeDtypeStruct(pair, jnp.float32)]
        + [jax.ShapeDtypeStruct(pair, jnp.bfloat16)] * SPAN,
        scratch_shapes=[
            pltpu.VMEM((SPAN * rows_dev, 2 * rows_dev), jnp.float32),
            pltpu.VMEM((window, members * rows_dev), jnp.bfloat16),
            pltpu.VMEM((window, members * rows_dev), jnp.bfloat16),
        ],
        input_output_aliases=aliases,
        cost_estimate=pl.CostEstimate(
            flops=10 * elements * DH,
            bytes_accessed=4 * rows_dev * width * 2,
            transcendentals=elements,
        ),
        name="attention_back",
    )(*operands)


def product_kernel(*refs, sources, inner_size):
    x_refs = refs[:sources]
    kv_refs = refs[sources : 2 * sources]
    send_ref, keep_ref = refs[2 * sources :]
    mine = lax.axis_index("dp") % inner_size
    kv = jnp.concatenate([ref[...] for ref in kv_refs], axis=0)
    share = keep_ref.shape[0]

    def product(which):
        rows = jnp.concatenate([ref[which] for ref in x_refs], axis=1)
        return jnp.dot(rows, kv, preferred_element_type=jnp.float32)

    for turn in range(1, inner_size):
        send_ref[turn - 1] = product((mine + turn) % inner_size).astype(jnp.bfloat16)
    keep_ref[...] = product(mine)


def products(x_pieces, kv_pieces, inner_size):
    rows = x_pieces[0].shape[1]
    columns = kv_pieces[0].shape[1]
    vmem = pl.BlockSpec(memory_space=pltpu.VMEM)
    tokens = len(x_pieces) * x_pieces[0].shape[2]
    return pl.pallas_call(
        partial(product_kernel, sources=len(x_pieces), inner_size=inner_size),
        in_specs=[vmem] * (2 * len(x_pieces)),
        out_specs=[vmem, vmem],
        out_shape=[
            jax.ShapeDtypeStruct((max(inner_size - 1, 1), rows, columns), jnp.bfloat16),
            jax.ShapeDtypeStruct((rows, columns), jnp.float32),
        ],
        cost_estimate=pl.CostEstimate(
            flops=2 * inner_size * rows * columns * tokens,
            bytes_accessed=inner_size * rows * (tokens * 2 + columns * 4),
            transcendentals=0,
        ),
        name="row_products",
    )(*x_pieces, *kv_pieces)


def turn_kernel(*refs, received, lo_size, turns):
    keep_ref = refs[0]
    got_refs = refs[1 : 1 + received]
    out_refs = refs[1 + received :]
    place = lax.axis_index("attn") // lo_size
    share = keep_ref.shape[0] // turns
    for turn in range(turns):
        at = pl.ds(pl.multiple_of((place + turn) % turns * share, share), share)
        total = keep_ref[at, :]
        for ref in got_refs:
            total = total + ref[at, :].astype(jnp.float32)
        out_refs[turn][...] = total.astype(out_refs[turn].dtype)


def turned_sums(keep, got, lo_size, turns):
    rows, columns = keep.shape
    share = (rows // turns, columns)
    vmem = pl.BlockSpec(memory_space=pltpu.VMEM)
    return pl.pallas_call(
        partial(turn_kernel, received=len(got), lo_size=lo_size, turns=turns),
        in_specs=[vmem] * (1 + len(got)),
        out_specs=[vmem] * turns,
        out_shape=[jax.ShapeDtypeStruct(share, jnp.float32)]
        + [jax.ShapeDtypeStruct(share, jnp.bfloat16)] * (turns - 1),
        cost_estimate=pl.CostEstimate(
            flops=2 * rows * columns, bytes_accessed=8 * rows * columns, transcendentals=0
        ),
        name="turned_sums",
    )(keep, *got)


def shards(query_states, key_states, value_states, out_grad, doc_lengths, layer_inputs):
    rows_dev = query_states.shape[0]
    attn_size = lax.axis_size("attn")
    data_size = lax.axis_size("dp")
    grid = Grid(attn_size, data_size)
    key_width = key_states.shape[1]
    key_heads = key_width // DH
    feat_size = layer_inputs.shape[0]
    row_share = feat_size // (data_size * attn_size)
    norm_factor = float(rows_dev * attn_size * data_size) ** (-0.5)
    chunk_heads = key_heads // CHUNKS
    outer_at = lax.axis_index("dp") // grid.inner
    lo_at = lax.axis_index("attn") % grid.lo

    packed = jnp.concatenate(
        [
            side[:, h * DH : (h + 1) * DH]
            for h in range(key_heads)
            for side in (key_states, value_states)
        ],
        axis=1,
    )
    width = chunk_heads * 2 * DH
    kv_blocks = []
    for chunk in range(CHUNKS):
        own = packed[:, chunk * width : (chunk + 1) * width]
        kv_blocks.append(
            [own] + [passed_along(own, "attn", offset) for offset in range(1, SPAN + 1)]
        )

    viewed = layer_inputs.reshape(
        grid.outer, grid.inner, grid.hi, grid.lo, row_share, rows_dev
    )
    labels = [(a, b) for a in range(grid.outer) for b in range(grid.lo)]
    x_pieces = []
    for a, b in labels:
        piece = lax.dynamic_index_in_dim(viewed, (outer_at + a) % grid.outer, 0, False)
        piece = lax.dynamic_index_in_dim(piece, (lo_at + b) % grid.lo, 2, False)
        piece = piece.reshape(grid.inner, grid.hi * row_share, rows_dev)
        x_pieces.append(piece if a == b == 0 else grid.rotated(piece, outer=a, lo=b))

    query_grad = None
    sums = []
    for chunk in range(CHUNKS):
        query_grad, own, *parts = attention(
            chunk, doc_lengths, query_states, out_grad, kv_blocks[chunk], query_grad
        )
        total = own
        for offset in range(1, SPAN + 1):
            back = passed_along(parts[offset - 1], "attn", -offset)
            total = total + back.astype(jnp.float32)
        rows = total.astype(jnp.bfloat16)
        kv_pieces = {}
        for a, b in labels:
            if a == b == 0:
                kv_pieces[a, b] = rows
            elif b == 0:
                kv_pieces[a, b] = grid.rotated(rows, outer=a)
            else:
                kv_pieces[a, b] = grid.rotated(kv_pieces[a, 0], lo=b)
        send, keep = products(x_pieces, [kv_pieces[label] for label in labels], grid.inner)
        got = [grid.rotated(send[turn - 1], inner=turn) for turn in range(1, grid.inner)]
        mine, *others = turned_sums(keep, got, grid.lo, grid.hi)
        for turn in range(1, grid.hi):
            back = grid.rotated(others[turn - 1], hi=turn)
            mine = mine + back.astype(jnp.float32)
        sums.append(mine)
    total = jnp.concatenate(sums, axis=1) * norm_factor
    weight_grad = jnp.concatenate(
        [
            total[:, (2 * h + side) * DH : (2 * h + side + 1) * DH]
            for side in range(2)
            for h in range(key_heads)
        ],
        axis=1,
    )
    return (query_grad, weight_grad)


def solution(mesh):
    placed = (
        P(("dp", "attn"), None),
        P(("dp", "attn"), None),
        P(("dp", "attn"), None),
        P(("dp", "attn"), None),
        P("dp", None),
        P(None, ("dp", "attn")),
    )
    return jax.shard_map(
        shards,
        mesh=mesh,
        in_specs=placed,
        out_specs=(P(("dp", "attn"), None), P(("dp", "attn"), None)),
        check_vma=False,
    )
```

```python
from functools import partial, reduce

import jax
import jax.numpy as jnp
from jax import lax
from jax.experimental import pallas as pl
from jax.experimental.pallas import tpu as pltpu
from jax.sharding import PartitionSpec as P

DH = 128
SPAN = 3
LAST = 2
DIRECT = ()
STRIP = 16
LOG2E = 1.4426950408889634

masked_score = -1e30


VMEM = pl.BlockSpec(memory_space=pltpu.VMEM)
HBM = pl.BlockSpec(memory_space=pltpu.HBM)


def in_hbm(array):
    return pltpu.with_memory_space_constraint(array, pltpu.HBM)


def copied(pairs, sem):
    copies = [
        pltpu.make_async_copy(source, target, sem.at[at])
        for at, (source, target) in enumerate(pairs)
    ]
    for copy in copies:
        copy.start()
    for copy in copies:
        copy.wait()


def granted(mib):
    return pltpu.CompilerParams(vmem_limit_bytes=mib * 1024 * 1024)


class Grid:
    def __init__(self, attn_size, data_size):
        self.attn = attn_size
        self.data = data_size
        self.lo = 2 if attn_size % 2 == 0 else 1
        self.hi = attn_size // self.lo
        self.inner = 2 if data_size % 2 == 0 else 1
        self.outer = data_size // self.inner

    def index(self, outer, inner, hi, lo):
        return (outer * self.inner + inner) * self.attn + hi * self.lo + lo

    def flipped(self, value, bit):
        pairs = []
        for i in range(self.attn * self.data):
            data, attn = divmod(i, self.attn)
            hi, lo = divmod(attn, self.lo)
            pairs.append((i, data * self.attn + (hi ^ bit) * self.lo + lo))
        return lax.ppermute(value, ("dp", "attn"), pairs)

    def turned(self, place, step):
        if self.hi & (self.hi - 1):
            return (place + step) % self.hi
        return place ^ step

    def rotated(self, value, outer=0, inner=0, hi=0, lo=0):
        pairs = []
        for o in range(self.outer):
            for i in range(self.inner):
                for h in range(self.hi):
                    for l in range(self.lo):
                        target = self.index(
                            (o + outer) % self.outer,
                            (i + inner) % self.inner,
                            (h + hi) % self.hi,
                            (l + lo) % self.lo,
                        )
                        pairs.append((self.index(o, i, h, l), target))
        return lax.ppermute(value, ("dp", "attn"), pairs)


def attention_kernel(
    lengths, query_ref, grad_ref, *refs, first, heads, lo_size, rows_dev, members, score_scale
):
    own_kv, side_kv, back_kv, cross_kv = refs[:4]
    odd = (lax.axis_index("attn") % 2 == 1) | (lo_size == 1)
    dq_all, own_all = refs[-(SPAN + 8) : -(SPAN + 6)]
    part_alls = refs[-(SPAN + 6) : -6]
    bias_ref, near_ref, s_ref, d_ref, ds_ref, p_ref = refs[-6:]
    head_size = DH
    wide = 2 * rows_dev
    key_at = lax.broadcasted_iota(jnp.int32, (rows_dev, wide), 0)
    query_at = lax.broadcasted_iota(jnp.int32, (rows_dev, wide), 1) % rows_dev
    causal = key_at <= query_at

    def prepare():
        near_ref[...] = jnp.where(causal, 1.0, 0.0).astype(jnp.bfloat16)
        base = lax.axis_index("attn") * rows_dev
        start = jnp.zeros((rows_dev, wide), jnp.int32)
        bound = jnp.int32(0)
        for doc in range(lengths.shape[1]):
            bound = bound + lengths[0, doc]
            start = jnp.where(query_at + base >= bound, bound, start)
        start = start - base
        merged_at = jnp.where(causal, key_at, key_at - SPAN * rows_dev)
        bias_ref[0:rows_dev, :] = jnp.where(merged_at >= start, 0.0, masked_score)
        for offset in range(1, SPAN):
            visible = key_at - offset * rows_dev >= start
            bias_ref[offset * rows_dev : (offset + 1) * rows_dev, :] = jnp.where(
                visible, 0.0, masked_score
            )

    prepare()

    def one_head(h, carry):
        pair_at = pl.ds(pl.multiple_of(h * 2 * head_size, 2 * head_size), 2 * head_size)
        group = members * head_size
        group_at = pl.ds(pl.multiple_of((first + h) * group, group), group)
        q_ref, g_ref = query_ref.at[:, group_at], grad_ref.at[:, group_at]
        dq_ref = dq_all.at[:, pl.ds(pl.multiple_of(h * group, group), group)]
        own_ref = own_all.at[:, pair_at]
        part_refs = [ref.at[:, pair_at] for ref in part_alls]
        own, side, back, cross = (
            ref[:, pair_at] for ref in (own_kv, side_kv, back_kv, cross_kv)
        )
        kv_all = [own, jnp.where(odd, side, cross), back, jnp.where(odd, cross, side)]
        keys = jnp.concatenate([side[:, :head_size] for side in kv_all], axis=0)
        values = jnp.concatenate([side[:, head_size:] for side in kv_all], axis=0)
        keys_turned = keys.T
        last_dims = (((1,), (1,)), ((), ()))

        def head(ref, j):
            return ref[:, j * head_size : (j + 1) * head_size]

        def mixed(array):
            sides = (block(array, 0), block(array, SPAN))
            return jnp.concatenate(
                [side[at : at + STRIP] for at in range(0, rows_dev, STRIP) for side in sides], axis=0
            )

        def strips(mixture, array, right, offset):
            left = block(array, offset) if offset else mixture
            product = lax.dot_general(left, right, last_dims, preferred_element_type=jnp.float32)
            for at in range(0, rows_dev, STRIP):
                out = slice(offset * rows_dev + at, offset * rows_dev + at + STRIP)
                if offset:
                    yield out, product[at : at + STRIP]
                else:
                    near = product[2 * at : 2 * at + STRIP]
                    far = product[2 * at + STRIP : 2 * at + 2 * STRIP]
                    yield out, jnp.where(causal[at : at + STRIP], near, far)

        def rows_of(offset):
            return slice(offset * rows_dev, (offset + 1) * rows_dev)

        def block(array, offset):
            return array[rows_of(offset), :]

        mixed_keys, mixed_values = mixed(keys), mixed(values)
        for pair in range(members // 2):
            q_two = jnp.concatenate([head(q_ref, 2 * pair), head(q_ref, 2 * pair + 1)], axis=0)
            g_two = jnp.concatenate([head(g_ref, 2 * pair), head(g_ref, 2 * pair + 1)], axis=0)
            top = jnp.full((8, wide), 2 * masked_score, jnp.float32)
            for offset in range(SPAN):
                for at, s in strips(mixed_keys, keys, q_two, offset):
                    s = s + bias_ref[at, :]
                    s_ref[pair, at, :] = s
                    top = jnp.maximum(top, jnp.max(s.reshape(-1, 8, wide), axis=0))
            top = jnp.max(top, axis=0, keepdims=True)
            sums = jnp.zeros((8, wide), jnp.float32)
            weighted = jnp.zeros((8, wide), jnp.float32)
            for offset in range(SPAN):
                for at, d in strips(mixed_values, values, g_two, offset):
                    d_ref[pair, at, :] = d
                    e = jnp.exp2((s_ref[pair, at, :] - top) * (score_scale * LOG2E))
                    s_ref[pair, at, :] = e
                    sums = sums + jnp.sum(e.reshape(-1, 8, wide), axis=0)
                    weighted = weighted + jnp.sum((e * d).reshape(-1, 8, wide), axis=0)
            sums = [jnp.sum(sums, axis=0, keepdims=True)]
            weighted = [jnp.sum(weighted, axis=0, keepdims=True)]
            inverse = 1.0 / reduce(jnp.add, sums)
            delta = reduce(jnp.add, weighted) * inverse
            columns = slice(pair * wide, (pair + 1) * wide)
            for offset in range(SPAN):
                probs = s_ref[pair, rows_of(offset), :] * inverse
                ds = probs * (d_ref[pair, rows_of(offset), :] - delta)
                for target, full in ((ds_ref, ds), (p_ref, probs)):
                    low = full.astype(jnp.bfloat16)
                    if offset == 0:
                        near = low * near_ref[...]
                        target[rows_of(SPAN), columns] = low - near
                        low = near
                    target[rows_of(offset), columns] = low
            dq_turned = score_scale * jnp.dot(
                keys_turned, ds_ref[:, columns], preferred_element_type=jnp.float32
            )
            for k in range(2):
                j = 2 * pair + k
                dq_ref[:, j * head_size : (j + 1) * head_size] = dq_turned[
                    :, k * rows_dev : (k + 1) * rows_dev
                ].T.astype(jnp.bfloat16)

        q_all = jnp.concatenate([head(q_ref, j) for j in range(members)], axis=0)
        g_all = jnp.concatenate([head(g_ref, j) for j in range(members)], axis=0)
        dk = score_scale * jnp.dot(ds_ref[...], q_all, preferred_element_type=jnp.float32)
        dv = jnp.dot(p_ref[...], g_all, preferred_element_type=jnp.float32)
        own_ref[:, :head_size] = block(dk, 0)
        own_ref[:, head_size:] = block(dv, 0)
        for part, odd_at, even_at in zip(part_refs, (1, 2, 3), (3, 2, 1)):
            for at, full in ((0, dk), (head_size, dv)):
                odd_part, even_part = block(full, odd_at), block(full, even_at)
                part[:, at : at + head_size] = jnp.where(odd, odd_part, even_part).astype(
                    jnp.bfloat16
                )
        return carry

    lax.fori_loop(0, heads, one_head, 0, unroll=True)


def attention(first, key_heads, lengths, queries, out_grads, kv_blocks, lo_size):
    rows_dev, width = queries.shape
    chunk_heads = kv_blocks[0].shape[1] // (2 * DH)
    members = width // (key_heads * DH)
    in_specs = [pl.BlockSpec(memory_space=pltpu.SMEM)] + [VMEM] * (2 + len(kv_blocks))
    operands = [lengths, queries, out_grads, *kv_blocks]
    pair = (rows_dev, chunk_heads * 2 * DH)
    window = (SPAN + 1) * rows_dev
    elements = chunk_heads * members * rows_dev * window
    return pl.pallas_call(
        partial(
            attention_kernel,
            first=first,
            heads=chunk_heads,
            lo_size=lo_size,
            rows_dev=rows_dev,
            members=members,
            score_scale=DH ** (-0.5),
        ),
        in_specs=in_specs,
        out_specs=[VMEM] * (SPAN + 2),
        out_shape=[jax.ShapeDtypeStruct((rows_dev, chunk_heads * members * DH), jnp.bfloat16)]
        + [jax.ShapeDtypeStruct(pair, jnp.float32)]
        + [jax.ShapeDtypeStruct(pair, jnp.bfloat16)] * SPAN,
        scratch_shapes=[
            pltpu.VMEM((SPAN * rows_dev, 2 * rows_dev), jnp.float32),
            pltpu.VMEM((rows_dev, 2 * rows_dev), jnp.bfloat16),
            pltpu.VMEM((members // 2, SPAN * rows_dev, 2 * rows_dev), jnp.float32),
            pltpu.VMEM((members // 2, SPAN * rows_dev, 2 * rows_dev), jnp.float32),
            pltpu.VMEM((window, members * rows_dev), jnp.bfloat16),
            pltpu.VMEM((window, members * rows_dev), jnp.bfloat16),
        ],
        cost_estimate=pl.CostEstimate(
            flops=10 * elements * DH,
            bytes_accessed=4 * rows_dev * width * 2,
            transcendentals=elements,
        ),
        compiler_params=pltpu.CompilerParams(vmem_limit_bytes=16 * 1024 * 1024),
        name="attention_back",
    )(*operands)


def head_split(heads):
    last = max(heads * LAST // 4, 1) if heads > 1 else 0
    return [heads - last, last] if last else [heads]


def pack_kernel(k_ref, v_ref, *refs):
    out_refs, sems = refs[:-1], refs[-1]
    pairs = []
    first = 0
    for out in out_refs:
        heads = out.shape[1] // (2 * DH)
        for h in range(heads):
            at = (first + h) * DH
            for side, ref in enumerate((k_ref, v_ref)):
                to = (2 * h + side) * DH
                pairs.append((ref.at[:, at : at + DH], out.at[:, to : to + DH]))
        first = first + heads
    copied(pairs, sems)


def packed(keys, values):
    rows, width = keys.shape
    split = head_split(width // DH)
    return pl.pallas_call(
        pack_kernel,
        in_specs=[HBM, HBM],
        out_specs=[VMEM] * len(split),
        out_shape=[jax.ShapeDtypeStruct((rows, 2 * DH * h), keys.dtype) for h in split],
        scratch_shapes=[pltpu.SemaphoreType.DMA((2 * width // DH,))],
        cost_estimate=pl.CostEstimate(flops=0, bytes_accessed=8 * rows * width, transcendentals=0),
        compiler_params=granted(8),
        name="pack",
    )(in_hbm(keys), in_hbm(values))


def sort_kernel(x_ref, *out_refs, grid, labels, order):
    outer_at = lax.axis_index("dp") // grid.inner
    inner_at = lax.axis_index("dp") % grid.inner
    hi_at = lax.axis_index("attn") // grid.lo
    lo_at = lax.axis_index("attn") % grid.lo
    share = x_ref.shape[1]
    for (a, b), out in zip(labels, out_refs):
        for i in range(grid.inner):
            for h, step in enumerate(order):
                block = grid.index(
                    (outer_at + a) % grid.outer,
                    (inner_at + i) % grid.inner,
                    grid.turned(hi_at, step),
                    (lo_at + b) % grid.lo,
                )
                out[i, h * share : (h + 1) * share, :] = x_ref[block]


def sorted_rows(layer_inputs, grid, labels, order):
    feat, tokens = layer_inputs.shape
    share = feat // (grid.data * grid.attn)
    out = jax.ShapeDtypeStruct((grid.inner, grid.hi * share, tokens), layer_inputs.dtype)
    return pl.pallas_call(
        partial(sort_kernel, grid=grid, labels=labels, order=order),
        in_specs=[VMEM],
        out_specs=[VMEM] * len(labels),
        out_shape=[out] * len(labels),
        cost_estimate=pl.CostEstimate(flops=0, bytes_accessed=4 * feat * tokens, transcendentals=0),
        compiler_params=granted(8),
        name="sort",
    )(layer_inputs.reshape(-1, share, tokens))


def product_kernel(*refs, sources, inner, received):
    x_refs = refs[:sources]
    kv_refs = refs[sources : 2 * sources]
    got_refs = refs[2 * sources : 2 * sources + received]
    out_refs = refs[2 * sources + received :]
    kv = jnp.concatenate([ref[...] for ref in kv_refs], axis=0)
    first = 0
    for out in out_refs:
        at = slice(first, first + out.shape[0])
        first = first + out.shape[0]
        rows = jnp.concatenate([ref[inner, at, :] for ref in x_refs], axis=1)
        total = jnp.dot(rows, kv, preferred_element_type=jnp.float32)
        for ref in got_refs:
            total = total + ref[at, :].astype(jnp.float32)
        out[...] = total.astype(out.dtype)


def products(x_pieces, kv_pieces, inner, got, outs):
    rows, tokens = x_pieces[0].shape[1:]
    columns = kv_pieces[0].shape[1]
    sources = len(x_pieces)
    return pl.pallas_call(
        partial(product_kernel, sources=sources, inner=inner, received=len(got)),
        in_specs=[VMEM] * (2 * sources + len(got)),
        out_specs=[VMEM] * len(outs),
        out_shape=[jax.ShapeDtypeStruct((share, columns), kind) for share, kind in outs],
        cost_estimate=pl.CostEstimate(
            flops=2 * rows * columns * tokens * sources,
            bytes_accessed=2 * sources * tokens * (rows + columns) + 4 * rows * columns,
            transcendentals=0,
        ),
        compiler_params=granted(8),
    )(*x_pieces, *kv_pieces, *got)


def finish_kernel(*refs, counts, norm_factor):
    out_ref = refs[-1]
    width = out_ref.shape[1] // 2
    first = 0
    for chunk, terms in enumerate(counts):
        at = sum(counts[:chunk])
        mine, *others = refs[at : at + terms]
        heads = mine.shape[1] // (2 * DH)
        for h in range(heads):
            for side in range(2):
                columns = slice((2 * h + side) * DH, (2 * h + side + 1) * DH)
                total = mine[:, columns]
                for ref in others:
                    total = total + ref[:, columns].astype(jnp.float32)
                to = side * width + (first + h) * DH
                out_ref[:, to : to + DH] = total * norm_factor
        first = first + heads


def finished(pieces, norm_factor):
    rows = pieces[0][0].shape[0]
    columns = sum(piece[0].shape[1] for piece in pieces)
    flat = [piece for chunk in pieces for piece in chunk]
    return pl.pallas_call(
        partial(finish_kernel, counts=[len(p) for p in pieces], norm_factor=norm_factor),
        in_specs=[VMEM] * len(flat),
        out_specs=VMEM,
        out_shape=jax.ShapeDtypeStruct((rows, columns), jnp.float32),
        cost_estimate=pl.CostEstimate(
            flops=0, bytes_accessed=14 * rows * columns, transcendentals=0
        ),
        compiler_params=granted(8),
        name="finish",
    )(*flat)


def join_kernel(*refs):
    part_refs, out_ref, sems = refs[:-2], refs[-2], refs[-1]
    pairs = []
    first = 0
    for ref in part_refs:
        pairs.append((ref, out_ref.at[:, first : first + ref.shape[1]]))
        first = first + ref.shape[1]
    copied(pairs, sems)


def joined(parts):
    rows = parts[0].shape[0]
    width = sum(part.shape[1] for part in parts)
    return pl.pallas_call(
        join_kernel,
        in_specs=[VMEM] * len(parts),
        out_specs=pl.BlockSpec(memory_space=pl.ANY),
        out_shape=jax.ShapeDtypeStruct((rows, width), parts[0].dtype),
        scratch_shapes=[pltpu.SemaphoreType.DMA((len(parts),))],
        cost_estimate=pl.CostEstimate(flops=0, bytes_accessed=4 * rows * width, transcendentals=0),
        compiler_params=granted(8),
        name="join",
    )(*parts)


def steps(pairs, size, keep):
    return [(i, j) for i, j in ((i, pairs(i)) for i in range(size) if keep(i)) if 0 <= j < size]


def every(i):
    return True


def odd(i):
    return i % 2 == 1


def swapped(i):
    return i ^ 1


def fetch(own, size, lo, chunk):
    if lo == 1:
        return [own] + [
            lax.ppermute(own, "attn", steps(lambda i: i + by, size, every))
            for by in range(1, SPAN + 1)
        ]
    back = lax.ppermute(own, "attn", steps(lambda i: i + 2, size, every))
    side = lax.ppermute(own, "attn", steps(lambda i: i + (3 if odd(i) else 1), size, every))
    if chunk in DIRECT:
        ahead = steps(lambda i: i + (1 if odd(i) else 3), size, every)
        cross = lax.ppermute(own, "attn", ahead)
    else:
        cross = lax.ppermute(back, "attn", steps(swapped, size, every))
    return [own, side, back, cross]


def give_back(own, parts, size, lo):
    wide, kind = jnp.float32, parts[0].dtype
    if lo == 1:
        total = own
        for by in range(1, SPAN + 1):
            got = lax.ppermute(parts[by - 1], "attn", steps(lambda i: i - by, size, every))
            total = total + got.astype(wide)
        return total.astype(kind)
    side, back, cross = parts
    crossed = lax.ppermute(cross, "attn", steps(swapped, size, every))
    sided = lax.ppermute(side, "attn", steps(lambda i: i - (1 if odd(i) else 3), size, every))
    summed = (back.astype(wide) + crossed.astype(wide)).astype(kind)
    came = lax.ppermute(summed, "attn", steps(lambda i: i - 2, size, every))
    return (own + came.astype(wide) + sided.astype(wide)).astype(kind)


def shards(query_states, key_states, value_states, out_grad, doc_lengths, layer_inputs):
    rows_dev = query_states.shape[0]
    attn_size = lax.axis_size("attn")
    data_size = lax.axis_size("dp")
    grid = Grid(attn_size, data_size)
    norm_factor = float(rows_dev * attn_size * data_size) ** (-0.5)
    key_heads = key_states.shape[1] // DH
    split = head_split(key_heads)
    chunks = range(len(split))
    labels = [(a, b) for a in range(grid.outer) for b in range(grid.lo)]
    row_share = layer_inputs.shape[0] // (data_size * attn_size)
    paired = grid.hi & (grid.hi - 1) == 0
    order = list(range(grid.hi))

    own_blocks = packed(key_states, value_states)
    kv_blocks = [fetch(own_blocks[c], attn_size, grid.lo, c) for c in chunks]
    x_pieces = list(sorted_rows(layer_inputs, grid, labels, order))
    for at, (a, b) in enumerate(labels):
        if at:
            x_pieces[at] = grid.rotated(x_pieces[at], outer=a, lo=b)

    query_grads = []
    found = []
    for c in chunks:
        query_grad, *grads = attention(
            sum(split[:c]),
            key_heads,
            doc_lengths,
            query_states,
            out_grad,
            kv_blocks[c],
            grid.lo,
        )
        query_grads.append(query_grad)
        found.append(grads)
    pieces = []
    for c in chunks:
        rows = give_back(found[c][0], found[c][1:], attn_size, grid.lo)
        kv_pieces = {}
        for a, b in labels:
            if a == b == 0:
                kv_pieces[a, b] = rows
                continue
            kv_pieces[a, b] = grid.rotated(rows, outer=a, lo=b)
        kv_all = [kv_pieces[label] for label in labels]
        got = []
        whole = grid.hi * row_share
        for turn in range(1, grid.inner):
            outs = [(whole, jnp.bfloat16)]
            (other,) = products(x_pieces, kv_all, turn, [], outs)
            got.append(grid.rotated(other, inner=turn))
        if paired:
            outs = [(row_share, jnp.float32)] + [(row_share, jnp.bfloat16)] * (grid.hi - 1)
            mine, *others = products(x_pieces, kv_all, 0, got, outs)
            pieces.append([mine])
            for step, piece in zip(order[1:], others):
                pieces[-1].append(grid.flipped(piece, step))
        else:
            outs = [(row_share, jnp.float32)] + [(row_share, jnp.bfloat16)] * (grid.hi - 1)
            mine, *others = products(x_pieces, kv_all, 0, got, outs)
            pieces.append([mine])
            for turn in range(1, grid.hi):
                pieces[-1].append(grid.rotated(others[turn - 1], hi=turn))
    return (joined(query_grads), finished(pieces, norm_factor))


def solution(mesh):
    placed = (
        P(("dp", "attn"), None),
        P(("dp", "attn"), None),
        P(("dp", "attn"), None),
        P(("dp", "attn"), None),
        P("dp", None),
        P(None, ("dp", "attn")),
    )

    return jax.shard_map(
        shards,
        mesh=mesh,
        in_specs=placed,
        out_specs=(P(("dp", "attn"), None), P(("dp", "attn"), None)),
        check_vma=False,
    )
```
